32 devices in a mesh: groups: 2 (over x), section: 16 (over z, y, core).
Axes of the slice: x: 2, y: 2, z: 4, core: 2. Of those that a mesh axis runs over, the one named last changes fastest.
Arguments:
- micro: bfloat16 [32, 192, 1024], P(('groups', 'section')), parts along dimension 0, may hold values from -6 to 6
- segment: int32 [32, 192], P(('groups', 'section')), parts along dimension 0, may hold values from 0 to 3, as said below
- gain: bfloat16 [16, 1024], P('section'), may hold values from 0.099609375 to 1.8984375
- w_query: bfloat16 [16, 1024, 2048], P('section'), may hold values from -0.1875 to 0.1875
- w_key: bfloat16 [16, 1024, 1024], P('section'), may hold values from -0.1875 to 0.1875
- w_value: bfloat16 [16, 1024, 1024], P('section'), may hold values from -0.1875 to 0.1875
- w_out: bfloat16 [16, 2048, 1024], P('section'), may hold values from -0.125 to 0.125
Outputs:
- result: bfloat16 [32, 192, 1024], P(('groups', 'section')), parts along dimension 0
The draws below stay inside these ranges and needn't reach their ends.
There are 2 independent parts, one for each index of `groups`. The reference program is written for one: setup_inputs(seed, part) draws one part's arguments, and reference() takes and returns one part's arrays. A program takes and returns all parts, laid end to end along the dimension named above; an argument that names none is the same for every part. Nothing has to cross between parts.
Inputs may be any that keep to these rules, and one draw needn't show every extreme that they name: `segment`: in each micro-batch the ids never fall, each of the 4 pairs holds 24 to 96 consecutive tokens, and one pair holds exactly 96.
All inputs are finite; a program needn't handle non-finite values.
Results may differ from the reference program's by a relative error of at most 0.013.
Values may be sent and summed in bfloat16 or wider, within the bound.
A program may use at most 128 MiB of HBM per device.

```python
import jax
import jax.numpy as jnp
from jax import lax

D = 1024
HEADS = 16
KV_HEADS = 8
HD = 128
TOK_DEV = 192
TICKS = 4
SECTIONS = 16
MAX_LEN = 96
MIN_LEN = 24


def one_batch(key):
    first_key, second_key = jax.random.split(key)
    extra = TOK_DEV // 8
    cuts = jax.random.randint(first_key, (2,), 0, extra + 1)
    lower_cut = jnp.minimum(cuts[0], cuts[1])
    upper_cut = jnp.maximum(cuts[0], cuts[1])
    smaller = jnp.stack([lower_cut, upper_cut - lower_cut, extra - upper_cut]) + MIN_LEN
    longest_at = jax.random.randint(second_key, (), 0, 4)
    lengths = []
    for slot in range(4):
        before = smaller[min(slot, 2)]
        after = smaller[max(slot - 1, 0)]
        pick = jnp.where(slot < longest_at, before, jnp.where(slot == longest_at, MAX_LEN, after))
        lengths.append(pick.astype(jnp.int32))
    ends = jnp.cumsum(jnp.stack(lengths)).astype(jnp.int32)
    where_at = jnp.arange(TOK_DEV, dtype=jnp.int32)
    return jnp.sum((where_at[:, None] >= ends[None, :3]).astype(jnp.int32), axis=1).astype(jnp.int32)


def draw_segment(key, part):
    keys = jax.random.split(key, SECTIONS)
    return jax.vmap(one_batch)(keys)


def steps_of(stream_key, dims, shards, least, high):
    loudness = 1.0
    for dim, shards_of in shards:
        steps = jax.random.uniform(jax.random.fold_in(jax.random.fold_in(stream_key, 6), dim), (shards_of,), jnp.float32, least / len(shards), high / len(shards))
        loudness = loudness * jnp.repeat(jnp.exp(steps), dims[dim] // shards_of).reshape((-1,) + (1,) * (len(dims) - 1 - dim))
    return loudness


def normal_values(key, extent, width, reach, pieces=(), held_as=jnp.bfloat16):
    factor_of = steps_of(key, extent, pieces, -0.22, 0.18) if pieces else 1.0
    values = jax.random.normal(key, extent, jnp.float32) * width * factor_of
    return jnp.minimum(jnp.maximum(values, -reach), reach).astype(held_as)


def setup_inputs(seed: int = 0, part: int = 0) -> dict:
    key_list = jax.random.split(jax.random.key(seed), 8)
    part_splits = jax.random.split(jax.random.fold_in(key_list[7], part), 8)
    micro = normal_values(part_splits[0], (SECTIONS, TOK_DEV, D), 1.0, 6.0, ((0, 16),))
    segment = draw_segment(jax.random.fold_in(jax.random.fold_in(key_list[7], part), 71), part)
    gain = jnp.clip(1.0 + 0.18 * jax.random.normal(key_list[2], (SECTIONS, D), jnp.float32), 0.099609375, 1.8984375).astype(jnp.bfloat16)
    w_query = normal_values(key_list[3], (SECTIONS, D, HEADS * HD), D ** -0.5, 0.1875, ((0, 16),))
    w_key = normal_values(key_list[4], (SECTIONS, D, KV_HEADS * HD), D ** -0.5, 0.1875, ((0, 16),))
    w_value = normal_values(key_list[5], (SECTIONS, D, KV_HEADS * HD), D ** -0.5, 0.1875, ((0, 16),))
    w_out = normal_values(key_list[6], (SECTIONS, HEADS * HD, D), (HEADS * HD) ** -0.5, 0.125, ((0, 16),))
    return {"micro": micro, "segment": segment, "gain": gain, "w_query": w_query, "w_key": w_key, "w_value": w_value, "w_out": w_out}


def positions(pair_ids):
    length = pair_ids.shape[0]
    matched = pair_ids[:, None] == pair_ids[None, :]
    row_index = lax.broadcasted_iota(jnp.int32, (length, length), 0)
    column = lax.broadcasted_iota(jnp.int32, (length, length), 1)
    earlier = matched & (column < row_index)
    places = lax.optimization_barrier(jnp.sum(earlier.astype(jnp.float32), axis=1))
    allowed = matched & (column <= row_index)
    return (places, allowed)

def rotate(values, places):
    middle = values.shape[2] // 2
    ladder = jnp.arange(middle, dtype=jnp.float32)
    spacing = 1000000.0 ** (-2.0 * ladder / (2 * middle))
    angles = places[:, None, None] * spacing[None, None, :]
    cosine = jnp.cos(angles)
    sine_part = jnp.sin(angles)
    front_part = values[:, :, :middle]
    second = values[:, :, middle:]
    return jnp.concatenate([front_part * cosine - second * sine_part, second * cosine + front_part * sine_part], axis=2)

def apply_layer(stream, pair_ids, gain_row, wq_layer, wk_layer, wv_layer, wo_layer):
    length = stream.shape[0]
    stream_f = stream.astype(jnp.float32)
    scale = lax.rsqrt(lax.optimization_barrier(jnp.mean(stream_f * stream_f, axis=1, keepdims=True)) + 1e-05)
    normed = (stream_f * scale * gain_row.astype(jnp.float32)[None, :]).astype(jnp.bfloat16)
    places, allowed = positions(pair_ids)
    queries = rotate(jnp.dot(normed, wq_layer, preferred_element_type=jnp.float32).reshape(length, HEADS, HD), places).astype(jnp.bfloat16)
    key_rows = rotate(jnp.dot(normed, wk_layer, preferred_element_type=jnp.float32).reshape(length, KV_HEADS, HD), places).astype(jnp.bfloat16)
    value_rows = jnp.dot(normed, wv_layer, preferred_element_type=jnp.float32).reshape(length, KV_HEADS, HD).astype(jnp.bfloat16)
    grouped = queries.reshape(length, KV_HEADS, HEADS // KV_HEADS, HD)
    scores = jnp.einsum('ikgd,jkd->kgij', grouped.astype(jnp.float32), key_rows.astype(jnp.float32)) * HD ** (-0.5)
    expo = jnp.where(allowed[None, None], jnp.exp(scores), jnp.zeros_like(scores))
    totals = lax.optimization_barrier(jnp.sum(expo, axis=3, keepdims=True))
    shares = (expo / totals).astype(jnp.bfloat16)
    mixed = jnp.einsum('kgij,jkd->ikgd', shares.astype(jnp.float32), value_rows.astype(jnp.float32)).astype(jnp.bfloat16)
    mixed = mixed.reshape(length, HEADS * HD)
    return (stream_f + jnp.dot(mixed, wo_layer, preferred_element_type=jnp.float32)).astype(jnp.bfloat16)

def reference(micro, segment, gain, w_query, w_key, w_value, w_out):

    def one_section(section_now):
        anchor = (section_now - (TICKS - 1)) % SECTIONS
        stream = micro[anchor]
        pair_ids = segment[anchor]
        for tick_index in range(TICKS):
            layer_at = (anchor + tick_index) % SECTIONS
            stream = apply_layer(stream, pair_ids, gain[layer_at], w_query[layer_at], w_key[layer_at], w_value[layer_at], w_out[layer_at])
        return stream
    return lax.map(one_section, jnp.arange(SECTIONS, dtype=jnp.int32))
```

```python
import functools
import math

import jax
import jax.numpy as jnp
import numpy as np
from jax import lax
from jax.experimental import pallas as pl
from jax.experimental.pallas import tpu as pltpu
from jax.sharding import PartitionSpec as P

HD = 128
TICKS = 4
PIECES = 4
BAND = 96
PAIRS = 4
MESH = pl.DeviceIdType.MESH
FOLD = HD ** -0.5 * math.log2(math.e)


def rope_table(length):
    spacing = 1000000.0 ** (-2.0 * np.arange(HD // 2) / HD)
    angles = np.arange(length)[:, None] * spacing[None, :]
    cosine, sine = np.cos(angles), np.sin(angles)
    full = np.concatenate([cosine, cosine, -sine, sine], axis=1).astype(np.float32)
    high = full.astype(jnp.bfloat16)
    low = (full - high.astype(np.float32)).astype(jnp.bfloat16)
    return np.concatenate([high, low], axis=1)


def blocks_of(length):
    rows = 128 - BAND
    later = [(r, r + rows, r - BAND, r + rows) for r in range(128, length, rows)]
    return [(0, 128, 0, 128)] + later


def kernel(
    length, width,
    micro, ids, gain_hbm, table_hbm, wq, wk, wv, wo, out,
    xbuf, ybuf, idbuf, gain, table, wqkv, wout,
    normed, acc, oacc, qs, kd, vd, mixed, turns, cosq, sinq, cosk, sink, scale, squares, bias,
    wsem, osem, lsem, send, recv, id_send, id_recv,
):
    n = lax.axis_size("section")
    me = lax.axis_index("section")
    right, left = lax.rem(me + 1, n), lax.rem(me + n - 1, n)
    piece = width // PIECES
    f32, bf = jnp.float32, jnp.bfloat16

    def local(src, dst, sem):
        return pltpu.make_async_copy(src, dst, sem)

    small = [
        local(ids, idbuf.at[0], lsem.at[0]),
        local(table_hbm, table, lsem.at[1]),
        local(micro.at[0], xbuf.at[0], lsem.at[2]),
        local(gain_hbm, gain, lsem.at[3]),
    ]
    for copy in small:
        copy.start()

    def pair_copies(j):
        q_at = pl.ds(j * 4 * HD, 4 * HD)
        k_at = pl.ds(j * 2 * HD, 2 * HD)
        return (
            local(wq.at[0, :, q_at], wqkv.at[j, :, 0 : 4 * HD], wsem.at[j, 0]),
            local(wk.at[0, :, k_at], wqkv.at[j, :, 4 * HD : 6 * HD], wsem.at[j, 1]),
            local(wv.at[0, :, k_at], wqkv.at[j, :, 6 * HD :], wsem.at[j, 2]),
        )

    def out_copy(p):
        at = pl.ds(p * piece, piece)
        return local(wo.at[0, :, at], wout.at[:, at], osem.at[p])

    for j in range(2):
        for copy in pair_copies(j):
            copy.start()

    barrier = pltpu.get_barrier_semaphore()
    pl.semaphore_signal(barrier, inc=1, device_id={"section": left}, device_id_type=MESH)
    pl.semaphore_wait(barrier, 1)
    for h in range(2):
        kd[:, h, :, (1 - h) * HD : (2 - h) * HD] = jnp.zeros((PAIRS, length, HD), bf)
        vd[:, h, :, (1 - h) * HD : (2 - h) * HD] = jnp.zeros((PAIRS, length, HD), bf)
    for copy in small:
        copy.wait()

    def piece_copy(t, p):
        at = pl.ds(p * piece, piece)
        return pltpu.make_async_remote_copy(
            ybuf.at[t, :, at], xbuf.at[t + 1, :, at], send.at[t, p], recv.at[t, p],
            device_id={"section": right}, device_id_type=MESH,
        )

    def id_copy(t):
        return pltpu.make_async_remote_copy(
            idbuf.at[t], idbuf.at[t + 1], id_send.at[t], id_recv.at[t],
            device_id={"section": right}, device_id_type=MESH,
        )

    def places(t):
        row = idbuf[t].astype(f32)
        i = lax.broadcasted_iota(jnp.int32, (length, length), 0)
        j = lax.broadcasted_iota(jnp.int32, (length, length), 1)
        across = jnp.broadcast_to(row, (length, length))
        down = jnp.sum(jnp.where(i == j, across, 0.0), axis=1, keepdims=True)
        matched = across == down
        place = jnp.sum(jnp.where(matched & (j < i), 1.0, 0.0), axis=1, keepdims=True)
        chosen = jnp.where(j.astype(f32) == place, 1.0, 0.0).astype(bf)
        made = jnp.dot(chosen, table[...], preferred_element_type=f32)
        turns[:, :HD] = made[:, :HD] + made[:, 2 * HD : 3 * HD]
        turns[:, HD:] = made[:, HD : 2 * HD] + made[:, 3 * HD :]
        limits = jnp.where(matched & (j <= i), 0.0, -1e30)
        for r0, r1, k0, k1 in blocks_of(length):
            bias[r0:r1, 0 : k1 - k0] = limits[r0:r1, k0:k1]

    def weigh(t, p):
        at = slice(p * piece, (p + 1) * piece)
        x = xbuf[t, :, at].astype(f32)
        normed[:, at] = (x * gain[:, at].astype(f32)).astype(bf)
        s = x * x
        s = sum(s[:, c : c + HD] for c in range(0, piece, HD))
        if p == 0:
            squares[...] = s
        else:
            squares[...] += s

    def rescale():
        mean = jnp.sum(squares[...], axis=1, keepdims=True) * (1.0 / width)
        s = jnp.broadcast_to(lax.rsqrt(mean + 1e-05), (length, HD))
        scale[...] = s
        c, d = turns[:, :HD] * s, turns[:, HD:] * s
        cosk[...] = c
        sink[...] = d
        cosq[...] = c * FOLD
        sinq[...] = d * FOLD

    def turn_q(x):
        return (x * cosq[...] + pltpu.roll(x, HD // 2, 1) * sinq[...]).astype(bf)

    def turn_k(x):
        return (x * cosk[...] + pltpu.roll(x, HD // 2, 1) * sink[...]).astype(bf)

    def product(j, c, k0, k1):
        return jnp.dot(
            normed[:, k0:k1], wqkv[j, k0:k1, c * 2 * HD : (c + 1) * 2 * HD], preferred_element_type=f32
        )

    def gather(j, k0, k1, start):
        for c in range(4):
            at = slice(c * 2 * HD, (c + 1) * 2 * HD)
            if start:
                acc[j, :, at] = product(j, c, k0, k1)
            else:
                acc[j, :, at] += product(j, c, k0, k1)

    def keep(j, k0, k1):
        for c in range(4):
            made = product(j, c, k0, k1)
            if k0:
                made += acc[j, :, c * 2 * HD : (c + 1) * 2 * HD]
            a, b = made[:, :HD], made[:, HD:]
            if c < 2:
                at = slice(c * HD, (c + 1) * HD)
                qs[j, 0, :, at] = turn_q(a)
                qs[j, 1, :, at] = turn_q(b)
            elif c == 2:
                kd[j, 0, :, :HD] = turn_k(a)
                kd[j, 1, :, HD:] = turn_k(b)
            else:
                vd[j, 0, :, :HD] = (a * scale[...]).astype(bf)
                vd[j, 1, :, HD:] = (b * scale[...]).astype(bf)

    def score(j):
        made = []
        for r0, r1, k0, k1 in blocks_of(length):
            count = r1 - r0
            q = qs[j, :, r0:r1, :].reshape(2 * count, 2 * HD)
            keys = kd[j, :, k0:k1, :].reshape(2 * HD, 2 * HD)
            scores = lax.dot_general(q, keys, (((1,), (1,)), ((), ())), preferred_element_type=f32)
            limit = bias[r0:r1, :]
            limit = jnp.concatenate([limit, limit], axis=0)
            parts = []
            for h in range(2):
                expo = jnp.exp2(scores[:, h * HD : (h + 1) * HD] + limit)
                parts.append((expo * pl.reciprocal(jnp.sum(expo, axis=1, keepdims=True))).astype(bf))
            made.append(jnp.concatenate(parts, axis=1))
        return made

    def mix(j, made):
        for (r0, r1, k0, k1), shares in zip(blocks_of(length), made):
            count = r1 - r0
            values = vd[j, :, k0:k1, :].reshape(2 * HD, 2 * HD)
            got = jnp.dot(shares, values, preferred_element_type=f32).astype(bf)
            for g in range(2):
                for h in range(2):
                    at = (4 * j + 2 * g + h) * HD
                    mixed[r0:r1, at : at + HD] = got[h * count : (h + 1) * count, g * HD : (g + 1) * HD]

    def spread(j):
        at = slice(j * 4 * HD, (j + 1) * 4 * HD)
        for p in range(PIECES):
            cols = slice(p * piece, (p + 1) * piece)
            made = jnp.dot(mixed[:, at], wout[at, cols], preferred_element_type=f32)
            if j == 0:
                oacc[:, cols] = made
            else:
                oacc[:, cols] += made

    def finish(t, p, start):
        cols = slice(p * piece, (p + 1) * piece)
        update = jnp.dot(mixed[:, start:], wout[start:, cols], preferred_element_type=f32)
        if start:
            update += oacc[:, cols]
        ybuf[t, :, cols] = (xbuf[t, :, cols].astype(f32) + update).astype(bf)

    id_copy(0).start()
    places(0)
    for p in range(PIECES):
        weigh(0, p)
    rescale()
    def arrive(j):
        for copy in pair_copies(j):
            copy.wait()

    made = {}
    for j in range(PAIRS):
        arrive(j)
        if j < 2:
            for copy in pair_copies(j + 2):
                copy.start()
        else:
            for p in (2 * j - 4, 2 * j - 3):
                out_copy(p).start()
        keep(j, 0, width)
        if j > 1:
            mix(j - 2, made.pop(j - 2))
        if j:
            made[j - 1] = score(j - 1)
    mix(PAIRS - 2, made.pop(PAIRS - 2))
    mix(PAIRS - 1, score(PAIRS - 1))
    for p in range(PIECES):
        out_copy(p).wait()
        finish(0, p, 0)
        piece_copy(0, p).start()

    steps = ((0, 2 * piece), (2 * piece, 3 * piece), (3 * piece, width))

    def later(t, carry):
        id_copy(t - 1).wait_recv()

        @pl.when(t < TICKS - 1)
        def _():
            id_copy(t).start()

        places(t)
        for k0, k1 in steps:
            for p in range(k0 // piece, k1 // piece):
                piece_copy(t - 1, p).wait_recv()
                weigh(t, p)
            if k1 < width:
                for j in range(PAIRS):
                    gather(j, k0, k1, k0 == 0)
        rescale()
        k0, k1 = steps[-1]
        keep(0, k0, k1)
        keep(1, k0, k1)
        made0 = score(0)
        keep(2, k0, k1)
        mix(0, made0)
        made1 = score(1)
        keep(3, k0, k1)
        mix(1, made1)
        spread(0)
        made2 = score(2)
        spread(1)
        mix(2, made2)
        made3 = score(3)
        spread(2)
        mix(3, made3)
        for p in range(PIECES):
            finish(t, p, (PAIRS - 1) * 4 * HD)
            pl.when(t < TICKS - 1)(piece_copy(t, p).start)
        return carry

    lax.fori_loop(1, TICKS, later, 0)
    out[0] = ybuf[TICKS - 1]
    for t in range(TICKS - 1):
        id_copy(t).wait_send()
        for p in range(PIECES):
            piece_copy(t, p).wait_send()


def body(micro, segment, gain, w_query, w_key, w_value, w_out):
    _, length, width = micro.shape
    table = jnp.asarray(rope_table(length))
    bf, f32 = jnp.bfloat16, jnp.float32
    any_space = pl.BlockSpec(memory_space=pl.ANY)
    vmem = pl.BlockSpec(memory_space=pltpu.VMEM)
    return pl.pallas_call(
        functools.partial(kernel, length, width),
        out_shape=jax.ShapeDtypeStruct((1, length, width), bf),
        in_specs=[any_space] * 8,
        out_specs=vmem,
        scratch_shapes=[
            pltpu.VMEM((TICKS, length, width), bf),
            pltpu.VMEM((TICKS, length, width), bf),
            pltpu.VMEM((TICKS, 1, length), jnp.int32),
            pltpu.VMEM((1, width), bf),
            pltpu.VMEM(table.shape, bf),
            pltpu.VMEM((PAIRS, width, 8 * HD), bf),
            pltpu.VMEM((PAIRS * 4 * HD, width), bf),
            pltpu.VMEM((length, width), bf),
            pltpu.VMEM((PAIRS, length, 8 * HD), f32),
            pltpu.VMEM((length, width), f32),
            pltpu.VMEM((PAIRS, 2, length, 2 * HD), bf),
            pltpu.VMEM((PAIRS, 2, length, 2 * HD), bf),
            pltpu.VMEM((PAIRS, 2, length, 2 * HD), bf),
            pltpu.VMEM((length, PAIRS * 4 * HD), bf),
            pltpu.VMEM((length, 2 * HD), f32),
            pltpu.VMEM((length, HD), f32),
            pltpu.VMEM((length, HD), f32),
            pltpu.VMEM((length, HD), f32),
            pltpu.VMEM((length, HD), f32),
            pltpu.VMEM((length, HD), f32),
            pltpu.VMEM((length, HD), f32),
            pltpu.VMEM((length, HD), f32),
            pltpu.SemaphoreType.DMA((PAIRS, 3)),
            pltpu.SemaphoreType.DMA((PIECES,)),
            pltpu.SemaphoreType.DMA((4,)),
            pltpu.SemaphoreType.DMA((TICKS - 1, PIECES)),
            pltpu.SemaphoreType.DMA((TICKS - 1, PIECES)),
            pltpu.SemaphoreType.DMA((TICKS - 1,)),
            pltpu.SemaphoreType.DMA((TICKS - 1,)),
        ],
        compiler_params=pltpu.CompilerParams(
            collective_id=0, has_side_effects=True, vmem_limit_bytes=60 * 1024 * 1024
        ),
    )(micro, segment, gain, table, w_query, w_key, w_value, w_out)


def solution(mesh):
    in_specs = (
        P(("groups", "section"), None, None),
        P(("groups", "section"), None),
        P("section", None),
        P("section", None, None),
        P("section", None, None),
        P("section", None, None),
        P("section", None, None),
    )
    out_specs = P(("groups", "section"), None, None)
    return jax.shard_map(body, mesh=mesh, in_specs=in_specs, out_specs=out_specs, check_vma=False)
```

```python
import functools
import math

import jax
import jax.numpy as jnp
import numpy as np
from jax import lax
from jax.experimental import pallas as pl
from jax.experimental.pallas import tpu as pltpu
from jax.sharding import PartitionSpec as P

HD = 128
TICKS = 4
PIECES = 4
BAND = 96
PAIRS = 4
MESH = pl.DeviceIdType.MESH
FOLD = HD ** -0.5 * math.log2(math.e)


def rope_table(length):
    spacing = 1000000.0 ** (-2.0 * np.arange(HD // 2) / HD)
    angles = np.arange(length)[:, None] * spacing[None, :]
    cosine, sine = np.cos(angles), np.sin(angles)
    full = np.concatenate([cosine, cosine, -sine, sine], axis=1).astype(np.float32)
    high = full.astype(jnp.bfloat16)
    low = (full - high.astype(np.float32)).astype(jnp.bfloat16)
    return np.concatenate([high, low], axis=1)


def blocks_of(length):
    rows = 128 - BAND
    later = [(r, r + rows, r - BAND, r + rows) for r in range(128, length, rows)]
    return [(0, 128, 0, 128)] + later


def kernel(
    length, width,
    micro, ids, gain_hbm, table_hbm, wq, wk, wv, wo, out,
    xbuf, ybuf, idbuf, gain, table, wqkv, wout,
    normed, acc, oacc, qs, kd, vd, mixed, turns, cosq, sinq, cosk, sink, scale, squares, bias,
    wsem, osem, lsem, send, recv, id_send, id_recv,
):
    n = lax.axis_size("section")
    me = lax.axis_index("section")
    right, left = lax.rem(me + 1, n), lax.rem(me + n - 1, n)
    piece = width // PIECES
    f32, bf = jnp.float32, jnp.bfloat16

    def local(src, dst, sem):
        return pltpu.make_async_copy(src, dst, sem)

    small = [
        local(ids, idbuf.at[0], lsem.at[0]),
        local(table_hbm, table, lsem.at[1]),
        local(micro.at[0], xbuf.at[0], lsem.at[2]),
        local(gain_hbm, gain, lsem.at[3]),
    ]
    for copy in small:
        copy.start()

    def pair_copies(j):
        q_at = pl.ds(j * 4 * HD, 4 * HD)
        k_at = pl.ds(j * 2 * HD, 2 * HD)
        return (
            local(wq.at[0, :, q_at], wqkv.at[j, :, 0 : 4 * HD], wsem.at[j, 0]),
            local(wk.at[0, :, k_at], wqkv.at[j, :, 4 * HD : 6 * HD], wsem.at[j, 1]),
            local(wv.at[0, :, k_at], wqkv.at[j, :, 6 * HD :], wsem.at[j, 2]),
        )

    def out_copy(p):
        at = pl.ds(p * piece, piece)
        return local(wo.at[0, :, at], wout.at[:, at], osem.at[p])

    def issue(j):
        for copy in pair_copies(j):
            copy.start()

    issue(0)
    issue(1)

    barrier = pltpu.get_barrier_semaphore()
    pl.semaphore_signal(barrier, inc=1, device_id={"section": left}, device_id_type=MESH)
    pl.semaphore_wait(barrier, 1)
    for h in range(2):
        kd[:, h, :, (1 - h) * HD : (2 - h) * HD] = jnp.zeros((PAIRS, length, HD), bf)
        vd[:, h, :, (1 - h) * HD : (2 - h) * HD] = jnp.zeros((PAIRS, length, HD), bf)
    for copy in small:
        copy.wait()

    def piece_copy(t, p):
        at = pl.ds(p * piece, piece)
        return pltpu.make_async_remote_copy(
            ybuf.at[t, :, at], xbuf.at[t + 1, :, at], send.at[t, p], recv.at[t, p],
            device_id={"section": right}, device_id_type=MESH,
        )

    def id_copy(t):
        return pltpu.make_async_remote_copy(
            idbuf.at[t], idbuf.at[t + 1], id_send.at[t], id_recv.at[t],
            device_id={"section": right}, device_id_type=MESH,
        )

    def places(t):
        row = idbuf[t].astype(f32)
        i = lax.broadcasted_iota(jnp.int32, (length, length), 0)
        j = lax.broadcasted_iota(jnp.int32, (length, length), 1)
        across = jnp.broadcast_to(row, (length, length))
        down = jnp.sum(jnp.where(i == j, across, 0.0), axis=1, keepdims=True)
        matched = across == down
        place = jnp.sum(jnp.where(matched & (j < i), 1.0, 0.0), axis=1, keepdims=True)
        chosen = jnp.where(j.astype(f32) == place, 1.0, 0.0).astype(bf)
        made = jnp.dot(chosen, table[...], preferred_element_type=f32)
        turns[:, :HD] = made[:, :HD] + made[:, 2 * HD : 3 * HD]
        turns[:, HD:] = made[:, HD : 2 * HD] + made[:, 3 * HD :]
        limits = jnp.where(matched & (j <= i), 0.0, -1e30)
        for r0, r1, k0, k1 in blocks_of(length):
            bias[r0:r1, 0 : k1 - k0] = limits[r0:r1, k0:k1]

    def weigh(t, p):
        at = slice(p * piece, (p + 1) * piece)
        x = xbuf[t, :, at].astype(f32)
        normed[:, at] = (x * gain[:, at].astype(f32)).astype(bf)
        s = x * x
        s = sum(s[:, c : c + HD] for c in range(0, piece, HD))
        if p == 0:
            squares[...] = s
        else:
            squares[...] += s

    def rescale():
        mean = jnp.sum(squares[...], axis=1, keepdims=True) * (1.0 / width)
        s = jnp.broadcast_to(lax.rsqrt(mean + 1e-05), (length, HD))
        scale[...] = s
        c, d = turns[:, :HD] * s, turns[:, HD:] * s
        cosk[...] = c
        sink[...] = d
        cosq[...] = c * FOLD
        sinq[...] = d * FOLD

    def turn_q(x):
        return (x * cosq[...] + pltpu.roll(x, HD // 2, 1) * sinq[...]).astype(bf)

    def turn_k(x):
        return (x * cosk[...] + pltpu.roll(x, HD // 2, 1) * sink[...]).astype(bf)

    def product(j, c, k0, k1):
        return jnp.dot(
            normed[:, k0:k1], wqkv[j, k0:k1, c * 2 * HD : (c + 1) * 2 * HD], preferred_element_type=f32
        )

    def gather(j, k0, k1, start):
        for c in range(4):
            at = slice(c * 2 * HD, (c + 1) * 2 * HD)
            if start:
                acc[j, :, at] = product(j, c, k0, k1)
            else:
                acc[j, :, at] += product(j, c, k0, k1)

    def keep(j, k0, k1):
        for c in range(4):
            made = product(j, c, k0, k1)
            if k0:
                made += acc[j, :, c * 2 * HD : (c + 1) * 2 * HD]
            a, b = made[:, :HD], made[:, HD:]
            if c < 2:
                at = slice(c * HD, (c + 1) * HD)
                qs[j, 0, :, at] = turn_q(a)
                qs[j, 1, :, at] = turn_q(b)
            elif c == 2:
                kd[j, 0, :, :HD] = turn_k(a)
                kd[j, 1, :, HD:] = turn_k(b)
            else:
                vd[j, 0, :, :HD] = (a * scale[...]).astype(bf)
                vd[j, 1, :, HD:] = (b * scale[...]).astype(bf)

    def score(j):
        made = []
        for r0, r1, k0, k1 in blocks_of(length):
            count = r1 - r0
            q = qs[j, :, r0:r1, :].reshape(2 * count, 2 * HD)
            keys = kd[j, :, k0:k1, :].reshape(2 * HD, 2 * HD)
            scores = lax.dot_general(q, keys, (((1,), (1,)), ((), ())), preferred_element_type=f32)
            limit = bias[r0:r1, :]
            limit = jnp.concatenate([limit, limit], axis=0)
            parts = []
            for h in range(2):
                expo = jnp.exp2(scores[:, h * HD : (h + 1) * HD] + limit)
                parts.append((expo * pl.reciprocal(jnp.sum(expo, axis=1, keepdims=True))).astype(bf))
            made.append(jnp.concatenate(parts, axis=1))
        return made

    def mix(j, made):
        for (r0, r1, k0, k1), shares in zip(blocks_of(length), made):
            count = r1 - r0
            values = vd[j, :, k0:k1, :].reshape(2 * HD, 2 * HD)
            got = jnp.dot(shares, values, preferred_element_type=f32).astype(bf)
            for g in range(2):
                for h in range(2):
                    at = (4 * j + 2 * g + h) * HD
                    mixed[r0:r1, at : at + HD] = got[h * count : (h + 1) * count, g * HD : (g + 1) * HD]

    def spread(j):
        at = slice(j * 4 * HD, (j + 1) * 4 * HD)
        for p in range(PIECES):
            cols = slice(p * piece, (p + 1) * piece)
            made = jnp.dot(mixed[:, at], wout[at, cols], preferred_element_type=f32)
            if j == 0:
                oacc[:, cols] = made
            else:
                oacc[:, cols] += made

    def finish(t, p, start):
        cols = slice(p * piece, (p + 1) * piece)
        update = jnp.dot(mixed[:, start:], wout[start:, cols], preferred_element_type=f32)
        if start:
            update += oacc[:, cols]
        ybuf[t, :, cols] = (xbuf[t, :, cols].astype(f32) + update).astype(bf)

    id_copy(0).start()
    places(0)
    for p in range(PIECES):
        weigh(0, p)
    rescale()
    def arrive(j):
        for copy in pair_copies(j):
            copy.wait()

    arrive(0)
    issue(2)
    keep(0, 0, width)
    arrive(1)
    issue(3)
    out_copy(0).start()
    out_copy(1).start()
    out_copy(2).start()
    out_copy(3).start()
    keep(1, 0, width)
    made0 = score(0)
    arrive(2)
    keep(2, 0, width)
    mix(0, made0)
    made1 = score(1)
    arrive(3)
    keep(3, 0, width)
    made2 = score(2)
    mix(1, made1)
    made3 = score(3)
    mix(2, made2)
    mix(3, made3)
    out_copy(0).wait()
    out_copy(1).wait()
    out_copy(2).wait()
    out_copy(3).wait()
    finish(0, 0, 0)
    piece_copy(0, 0).start()
    finish(0, 1, 0)
    piece_copy(0, 1).start()
    finish(0, 2, 0)
    piece_copy(0, 2).start()
    finish(0, 3, 0)
    piece_copy(0, 3).start()

    even = lax.rem(me, 2) == 0

    def later(t, carry):
        id_copy(t - 1).wait_recv()

        @pl.when(t < TICKS - 1)
        def _():
            id_copy(t).start()

        places(t)
        @pl.when(even)
        def _():
            for k0, k1 in ((0, piece), (piece, 2 * piece), (2 * piece, 3 * piece)):
                for p in range(k0 // piece, k1 // piece):
                    piece_copy(t - 1, p).wait_recv()
                    weigh(t, p)
                for j in range(PAIRS):
                    gather(j, k0, k1, k0 == 0)
            for p in range(3, PIECES):
                piece_copy(t - 1, p).wait_recv()
            for p in range(3, PIECES):
                weigh(t, p)
            rescale()
            keep(0, 3 * piece, width)
            keep(1, 3 * piece, width)
            made0 = score(0)
            keep(2, 3 * piece, width)
            made1 = score(1)
            mix(0, made0)
            keep(3, 3 * piece, width)
            made2 = score(2)
            mix(1, made1)
            spread(0)
            made3 = score(3)
            spread(1)
            mix(2, made2)
            spread(2)
            mix(3, made3)
            for p in range(PIECES):
                finish(t, p, (PAIRS - 1) * 4 * HD)

        @pl.when(jnp.logical_not(even))
        def _():
            for p in range(PIECES):
                piece_copy(t - 1, p).wait_recv()
            for p in range(PIECES):
                weigh(t, p)
            rescale()
            keep(0, 0, width)
            keep(1, 0, width)
            made0 = score(0)
            keep(2, 0, width)
            made1 = score(1)
            mix(0, made0)
            keep(3, 0, width)
            made2 = score(2)
            mix(1, made1)
            spread(0)
            made3 = score(3)
            spread(1)
            mix(2, made2)
            spread(2)
            mix(3, made3)
            for p in range(PIECES):
                finish(t, p, (PAIRS - 1) * 4 * HD)

        @pl.when(t < TICKS - 1)
        def _():
            for p in range(PIECES):
                piece_copy(t, p).start()

        return carry

    lax.fori_loop(1, TICKS, later, 0)
    out[0] = ybuf[TICKS - 1]
    for t in range(TICKS - 1):
        id_copy(t).wait_send()
        for p in range(PIECES):
            piece_copy(t, p).wait_send()


def body(micro, segment, gain, w_query, w_key, w_value, w_out):
    _, length, width = micro.shape
    table = jnp.asarray(rope_table(length))
    bf, f32 = jnp.bfloat16, jnp.float32
    any_space = pl.BlockSpec(memory_space=pl.ANY)
    vmem = pl.BlockSpec(memory_space=pltpu.VMEM)
    return pl.pallas_call(
        functools.partial(kernel, length, width),
        out_shape=jax.ShapeDtypeStruct((1, length, width), bf),
        in_specs=[any_space] * 8,
        out_specs=vmem,
        scratch_shapes=[
            pltpu.VMEM((TICKS, length, width), bf),
            pltpu.VMEM((TICKS, length, width), bf),
            pltpu.VMEM((TICKS, 1, length), jnp.int32),
            pltpu.VMEM((1, width), bf),
            pltpu.VMEM(table.shape, bf),
            pltpu.VMEM((PAIRS, width, 8 * HD), bf),
            pltpu.VMEM((PAIRS * 4 * HD, width), bf),
            pltpu.VMEM((length, width), bf),
            pltpu.VMEM((PAIRS, length, 8 * HD), f32),
            pltpu.VMEM((length, width), f32),
            pltpu.VMEM((PAIRS, 2, length, 2 * HD), bf),
            pltpu.VMEM((PAIRS, 2, length, 2 * HD), bf),
            pltpu.VMEM((PAIRS, 2, length, 2 * HD), bf),
            pltpu.VMEM((length, PAIRS * 4 * HD), bf),
            pltpu.VMEM((length, 2 * HD), f32),
            pltpu.VMEM((length, HD), f32),
            pltpu.VMEM((length, HD), f32),
            pltpu.VMEM((length, HD), f32),
            pltpu.VMEM((length, HD), f32),
            pltpu.VMEM((length, HD), f32),
            pltpu.VMEM((length, HD), f32),
            pltpu.VMEM((length, HD), f32),
            pltpu.SemaphoreType.DMA((PAIRS, 3)),
            pltpu.SemaphoreType.DMA((PIECES,)),
            pltpu.SemaphoreType.DMA((4,)),
            pltpu.SemaphoreType.DMA((TICKS - 1, PIECES)),
            pltpu.SemaphoreType.DMA((TICKS - 1, PIECES)),
            pltpu.SemaphoreType.DMA((TICKS - 1,)),
            pltpu.SemaphoreType.DMA((TICKS - 1,)),
        ],
        compiler_params=pltpu.CompilerParams(
            collective_id=0, has_side_effects=True, vmem_limit_bytes=44 * 1024 * 1024
        ),
    )(*[pltpu.with_memory_space_constraint(a, pltpu.HBM) for a in (micro, segment, gain, table, w_query, w_key, w_value, w_out)])


def solution(mesh):
    in_specs = (
        P(("groups", "section"), None, None),
        P(("groups", "section"), None),
        P("section", None),
        P("section", None, None),
        P("section", None, None),
        P("section", None, None),
        P("section", None, None),
    )
    out_specs = P(("groups", "section"), None, None)
    return jax.shard_map(body, mesh=mesh, in_specs=in_specs, out_specs=out_specs, check_vma=False)
```

```python
import functools
import math

import jax
import jax.numpy as jnp
import numpy as np
from jax import lax
from jax.experimental import pallas as pl
from jax.experimental.pallas import tpu as pltpu
from jax.sharding import PartitionSpec as P

HD = 128
TICKS = 4
PIECES = 4
BAND = 96
PAIRS = 4
MESH = pl.DeviceIdType.MESH
FOLD = HD ** -0.5 * math.log2(math.e)


def rope_table(length):
    spacing = 1000000.0 ** (-2.0 * np.arange(HD // 2) / HD)
    angles = np.arange(length)[:, None] * spacing[None, :]
    cosine, sine = np.cos(angles), np.sin(angles)
    full = np.concatenate([cosine, cosine, -sine, sine], axis=1).astype(np.float32)
    high = full.astype(jnp.bfloat16)
    low = (full - high.astype(np.float32)).astype(jnp.bfloat16)
    return np.concatenate([high, low], axis=1)


def blocks_of(start, stop):
    rows = 128 - BAND
    if start == 0:
        return [(0, stop, 0, 128)]
    return [(r, r + rows, r + rows - 128, r + rows) for r in range(start, stop, rows)]


def kernel(
    length, width,
    micro, ids, gain_hbm, table_hbm, wq, wk, wv, wo, out,
    xbuf, ybuf, idbuf, gain, table, wqkv, wout,
    normed, oacc, qs, kd, vd, mixed, turns, cosq, sinq, cosk, sink, scale, bias,
    wsem, osem, lsem, send, recv, id_send, id_recv,
):
    n = lax.axis_size("section")
    me = lax.axis_index("section")
    right, left = lax.rem(me + 1, n), lax.rem(me + n - 1, n)
    piece = width // PIECES
    cut = length // 2
    halves = ((0, cut), (cut, length))
    blocks = [blocks_of(*rows) for rows in halves]
    f32, bf = jnp.float32, jnp.bfloat16

    def local(src, dst, sem):
        return pltpu.make_async_copy(src, dst, sem)

    small = [
        local(ids, idbuf.at[0], lsem.at[0]),
        local(table_hbm, table, lsem.at[1]),
        local(micro.at[0], xbuf.at[0], lsem.at[2]),
        local(gain_hbm, gain, lsem.at[3]),
    ]
    for copy in small:
        copy.start()

    def pair_copies(j):
        q_at = pl.ds(j * 4 * HD, 4 * HD)
        k_at = pl.ds(j * 2 * HD, 2 * HD)
        return (
            local(wq.at[0, :, q_at], wqkv.at[j, :, 0 : 4 * HD], wsem.at[j, 0]),
            local(wk.at[0, :, k_at], wqkv.at[j, :, 4 * HD : 6 * HD], wsem.at[j, 1]),
            local(wv.at[0, :, k_at], wqkv.at[j, :, 6 * HD :], wsem.at[j, 2]),
        )

    def out_copy(p):
        at = pl.ds(p * piece, piece)
        return local(wo.at[0, :, at], wout.at[:, at], osem.at[p])

    def issue(j):
        for copy in pair_copies(j):
            copy.start()

    issue(0)
    issue(1)

    barrier = pltpu.get_barrier_semaphore()
    pl.semaphore_signal(barrier, inc=1, device_id={"section": left}, device_id_type=MESH)
    pl.semaphore_wait(barrier, 1)
    kd[...] = jnp.zeros(kd.shape, bf)
    vd[...] = jnp.zeros(vd.shape, bf)
    for copy in small:
        copy.wait()

    def half_copy(t, h):
        at = slice(*halves[h])
        return pltpu.make_async_remote_copy(
            ybuf.at[t, at, :], xbuf.at[t + 1, at, :], send.at[t, h], recv.at[t, h],
            device_id={"section": right}, device_id_type=MESH,
        )

    def id_copy(t):
        return pltpu.make_async_remote_copy(
            idbuf.at[t], idbuf.at[t + 1], id_send.at[t], id_recv.at[t],
            device_id={"section": right}, device_id_type=MESH,
        )

    def places(t):
        row = idbuf[t].astype(f32)
        i = lax.broadcasted_iota(jnp.int32, (length, length), 0)
        j = lax.broadcasted_iota(jnp.int32, (length, length), 1)
        across = jnp.broadcast_to(row, (length, length))
        down = jnp.sum(jnp.where(i == j, across, 0.0), axis=1, keepdims=True)
        matched = across == down
        place = jnp.sum(jnp.where(matched & (j < i), 1.0, 0.0), axis=1, keepdims=True)
        chosen = jnp.where(j.astype(f32) == place, 1.0, 0.0).astype(bf)
        made = jnp.dot(chosen, table[...], preferred_element_type=f32)
        turns[:, :HD] = made[:, :HD] + made[:, 2 * HD : 3 * HD]
        turns[:, HD:] = made[:, HD : 2 * HD] + made[:, 3 * HD :]
        limits = jnp.where(matched & (j <= i), 0.0, -1e30)
        for r0, r1, k0, k1 in blocks[0] + blocks[1]:
            bias[r0:r1, :] = limits[r0:r1, k0:k1]

    def weigh(t, start, stop):
        rows = slice(start, stop)
        x = xbuf[t, rows, :].astype(f32)
        normed[rows, :] = (x * gain[...].astype(f32)).astype(bf)
        mean = jnp.sum(x * x, axis=1, keepdims=True) * (1.0 / width)
        s = jnp.broadcast_to(lax.rsqrt(mean + 1e-05), (stop - start, HD))
        scale[rows, :] = s
        c, d = turns[rows, :HD] * s, turns[rows, HD:] * s
        cosk[rows, :] = c
        sink[rows, :] = d
        cosq[rows, :] = c * FOLD
        sinq[rows, :] = d * FOLD

    def keep(j, start, stop):
        rows = slice(start, stop)

        def turn(x, cosine, sine):
            return (x * cosine[rows, :] + pltpu.roll(x, HD // 2, 1) * sine[rows, :]).astype(bf)

        for c in range(4):
            made = jnp.dot(
                normed[rows, :], wqkv[j, :, c * 2 * HD : (c + 1) * 2 * HD], preferred_element_type=f32
            )
            a, b = made[:, :HD], made[:, HD:]
            if c < 2:
                at = slice(c * HD, (c + 1) * HD)
                qs[j, 0, rows, at] = turn(a, cosq, sinq)
                qs[j, 1, rows, at] = turn(b, cosq, sinq)
            elif c == 2:
                kd[j, 0, rows, :HD] = turn(a, cosk, sink)
                kd[j, 1, rows, HD:] = turn(b, cosk, sink)
            else:
                vd[j, 0, rows, :HD] = (a * scale[rows, :]).astype(bf)
                vd[j, 1, rows, HD:] = (b * scale[rows, :]).astype(bf)

    def score(j, over):
        made = []
        for r0, r1, k0, k1 in over:
            count = r1 - r0
            q = qs[j, :, r0:r1, :].reshape(2 * count, 2 * HD)
            keys = kd[j, :, k0:k1, :].reshape(2 * HD, 2 * HD)
            scores = lax.dot_general(q, keys, (((1,), (1,)), ((), ())), preferred_element_type=f32)
            limit = bias[r0:r1, :]
            limit = jnp.concatenate([limit, limit], axis=0)
            parts = []
            for h in range(2):
                expo = jnp.exp2(scores[:, h * HD : (h + 1) * HD] + limit)
                parts.append((expo * pl.reciprocal(jnp.sum(expo, axis=1, keepdims=True))).astype(bf))
            made.append(jnp.concatenate(parts, axis=1))
        return made

    def mix(j, over, made):
        for (r0, r1, k0, k1), shares in zip(over, made):
            count = r1 - r0
            values = vd[j, :, k0:k1, :].reshape(2 * HD, 2 * HD)
            got = jnp.dot(shares, values, preferred_element_type=f32).astype(bf)
            for g in range(2):
                for h in range(2):
                    at = (4 * j + 2 * g + h) * HD
                    mixed[r0:r1, at : at + HD] = got[h * count : (h + 1) * count, g * HD : (g + 1) * HD]

    def spread(j, start, stop):
        rows, at = slice(start, stop), slice(j * 4 * HD, (j + 1) * 4 * HD)
        for p in range(PIECES):
            cols = slice(p * piece, (p + 1) * piece)
            made = jnp.dot(mixed[rows, at], wout[at, cols], preferred_element_type=f32)
            if j == 0:
                oacc[rows, cols] = made
            else:
                oacc[rows, cols] += made

    def finish(t, start, stop, first):
        rows = slice(start, stop)
        for p in range(PIECES):
            cols = slice(p * piece, (p + 1) * piece)
            update = jnp.dot(mixed[rows, first:], wout[first:, cols], preferred_element_type=f32)
            if first:
                update += oacc[rows, cols]
            ybuf[t, rows, cols] = (xbuf[t, rows, cols].astype(f32) + update).astype(bf)

    def arrive(j):
        for copy in pair_copies(j):
            copy.wait()

    both = blocks[0] + blocks[1]
    id_copy(0).start()
    places(0)
    weigh(0, 0, length)
    arrive(0)
    issue(2)
    keep(0, 0, length)
    arrive(1)
    issue(3)
    out_copy(0).start()
    out_copy(1).start()
    out_copy(2).start()
    out_copy(3).start()
    keep(1, 0, length)
    low0 = score(0, blocks[0])
    arrive(2)
    keep(2, 0, length)
    low1 = score(1, blocks[0])
    mix(0, blocks[0], low0)
    high0 = score(0, blocks[1])
    arrive(3)
    keep(3, 0, length)
    low2 = score(2, blocks[0])
    mix(1, blocks[0], low1)
    high1 = score(1, blocks[1])
    low3 = score(3, blocks[0])
    mix(2, blocks[0], low2)
    mix(3, blocks[0], low3)
    out_copy(0).wait()
    out_copy(1).wait()
    out_copy(2).wait()
    out_copy(3).wait()
    finish(0, *halves[0], 0)
    half_copy(0, 0).start()
    mix(0, blocks[1], high0)
    mix(1, blocks[1], high1)
    high2 = score(2, blocks[1])
    high3 = score(3, blocks[1])
    mix(2, blocks[1], high2)
    mix(3, blocks[1], high3)
    finish(0, *halves[1], 0)
    half_copy(0, 1).start()

    def later(t, carry):
        id_copy(t - 1).wait_recv()

        @pl.when(t < TICKS - 1)
        def _():
            id_copy(t).start()

        places(t)
        for h, (start, stop) in enumerate(halves):
            over = blocks[h]
            half_copy(t - 1, h).wait_recv()
            weigh(t, start, stop)
            keep(0, start, stop)
            keep(1, start, stop)
            made0 = score(0, over)
            keep(2, start, stop)
            mix(0, over, made0)
            made1 = score(1, over)
            keep(3, start, stop)
            mix(1, over, made1)
            spread(0, start, stop)
            made2 = score(2, over)
            spread(1, start, stop)
            mix(2, over, made2)
            made3 = score(3, over)
            spread(2, start, stop)
            mix(3, over, made3)
            finish(t, start, stop, (PAIRS - 1) * 4 * HD)
            pl.when(t < TICKS - 1)(half_copy(t, h).start)
        return carry

    lax.fori_loop(1, TICKS, later, 0)
    out[0] = ybuf[TICKS - 1]
    for t in range(TICKS - 1):
        id_copy(t).wait_send()
        for h in range(2):
            half_copy(t, h).wait_send()


def body(micro, segment, gain, w_query, w_key, w_value, w_out):
    _, length, width = micro.shape
    table = jnp.asarray(rope_table(length))
    bf, f32 = jnp.bfloat16, jnp.float32
    any_space = pl.BlockSpec(memory_space=pl.ANY)
    vmem = pl.BlockSpec(memory_space=pltpu.VMEM)
    return pl.pallas_call(
        functools.partial(kernel, length, width),
        out_shape=jax.ShapeDtypeStruct((1, length, width), bf),
        in_specs=[any_space] * 8,
        out_specs=vmem,
        scratch_shapes=[
            pltpu.VMEM((TICKS, length, width), bf),
            pltpu.VMEM((TICKS, length, width), bf),
            pltpu.VMEM((TICKS, 1, length), jnp.int32),
            pltpu.VMEM((1, width), bf),
            pltpu.VMEM(table.shape, bf),
            pltpu.VMEM((PAIRS, width, 8 * HD), bf),
            pltpu.VMEM((PAIRS * 4 * HD, width), bf),
            pltpu.VMEM((length, width), bf),
            pltpu.VMEM((length, width), f32),
            pltpu.VMEM((PAIRS, 2, length, 2 * HD), bf),
            pltpu.VMEM((PAIRS, 2, length, 2 * HD), bf),
            pltpu.VMEM((PAIRS, 2, length, 2 * HD), bf),
            pltpu.VMEM((length, PAIRS * 4 * HD), bf),
            pltpu.VMEM((length, 2 * HD), f32),
            pltpu.VMEM((length, HD), f32),
            pltpu.VMEM((length, HD), f32),
            pltpu.VMEM((length, HD), f32),
            pltpu.VMEM((length, HD), f32),
            pltpu.VMEM((length, HD), f32),
            pltpu.VMEM((length, HD), f32),
            pltpu.SemaphoreType.DMA((PAIRS, 3)),
            pltpu.SemaphoreType.DMA((PIECES,)),
            pltpu.SemaphoreType.DMA((4,)),
            pltpu.SemaphoreType.DMA((TICKS - 1, 2)),
            pltpu.SemaphoreType.DMA((TICKS - 1, 2)),
            pltpu.SemaphoreType.DMA((TICKS - 1,)),
            pltpu.SemaphoreType.DMA((TICKS - 1,)),
        ],
        compiler_params=pltpu.CompilerParams(
            collective_id=0, has_side_effects=True, vmem_limit_bytes=44 * 1024 * 1024
        ),
    )(*[pltpu.with_memory_space_constraint(a, pltpu.HBM) for a in (micro, segment, gain, table, w_query, w_key, w_value, w_out)])


def solution(mesh):
    in_specs = (
        P(("groups", "section"), None, None),
        P(("groups", "section"), None),
        P("section", None),
        P("section", None, None),
        P("section", None, None),
        P("section", None, None),
        P("section", None, None),
    )
    out_specs = P(("groups", "section"), None, None)
    return jax.shard_map(body, mesh=mesh, in_specs=in_specs, out_specs=out_specs, check_vma=False)
```

```python
import functools
import math

import jax
import jax.numpy as jnp
import numpy as np
from jax import lax
from jax.experimental import pallas as pl
from jax.experimental.pallas import tpu as pltpu
from jax.sharding import PartitionSpec as P

HD = 128
TICKS = 4
PIECES = 4
BAND = 96
PAIRS = 4
MESH = pl.DeviceIdType.MESH
FOLD = HD ** -0.5 * math.log2(math.e)


def rope_table(length):
    spacing = 1000000.0 ** (-2.0 * np.arange(HD // 2) / HD)
    angles = np.arange(length)[:, None] * spacing[None, :]
    cosine, sine = np.cos(angles), np.sin(angles)
    full = np.concatenate([cosine, cosine, -sine, sine], axis=1).astype(np.float32)
    high = full.astype(jnp.bfloat16)
    low = (full - high.astype(np.float32)).astype(jnp.bfloat16)
    return np.concatenate([high, low], axis=1)


def blocks_of(start, stop):
    rows = 128 - BAND
    if start == 0:
        return [(0, stop, 0, 128)]
    return [(r, r + rows, r + rows - 128, r + rows) for r in range(start, stop, rows)]


def kernel(
    length, width,
    micro, ids, gain_hbm, table_hbm, wq, wk, wv, wo, out,
    xbuf, ybuf, idbuf, gain, table, wqkv, wout,
    normed, oacc, qs, kd, vd, mixed, turns, cosq, sinq, cosk, sink, scale, bias,
    wsem, osem, lsem, send, recv, id_send, id_recv,
):
    n = lax.axis_size("section")
    me = lax.axis_index("section")
    right, left = lax.rem(me + 1, n), lax.rem(me + n - 1, n)
    piece = width // PIECES
    cut = length // 2
    halves = ((0, cut), (cut, length))
    blocks = [blocks_of(*rows) for rows in halves]
    f32, bf = jnp.float32, jnp.bfloat16

    def local(src, dst, sem):
        return pltpu.make_async_copy(src, dst, sem)

    small = [
        local(ids, idbuf.at[0], lsem.at[0]),
        local(table_hbm, table, lsem.at[1]),
        local(micro.at[0], xbuf.at[0], lsem.at[2]),
        local(gain_hbm, gain, lsem.at[3]),
    ]
    for copy in small:
        copy.start()

    def pair_copies(j):
        q_at = pl.ds(j * 4 * HD, 4 * HD)
        k_at = pl.ds(j * 2 * HD, 2 * HD)
        return (
            local(wq.at[0, :, q_at], wqkv.at[j, :, 0 : 4 * HD], wsem.at[j, 0]),
            local(wk.at[0, :, k_at], wqkv.at[j, :, 4 * HD : 6 * HD], wsem.at[j, 1]),
            local(wv.at[0, :, k_at], wqkv.at[j, :, 6 * HD :], wsem.at[j, 2]),
        )

    def out_copy(p):
        at = pl.ds(p * piece, piece)
        return local(wo.at[0, :, at], wout.at[:, at], osem.at[p])

    def issue(j):
        for copy in pair_copies(j):
            copy.start()

    issue(0)
    issue(1)

    barrier = pltpu.get_barrier_semaphore()
    pl.semaphore_signal(barrier, inc=1, device_id={"section": left}, device_id_type=MESH)
    kd[...] = jnp.zeros(kd.shape, bf)
    vd[...] = jnp.zeros(vd.shape, bf)
    for copy in small:
        copy.wait()

    def half_copy(t, h):
        at = slice(*halves[h])
        return pltpu.make_async_remote_copy(
            ybuf.at[t, at, :], xbuf.at[t + 1, at, :], send.at[t, h], recv.at[t, h],
            device_id={"section": right}, device_id_type=MESH,
        )

    def id_copy(t):
        return pltpu.make_async_remote_copy(
            idbuf.at[t], idbuf.at[t + 1], id_send.at[t], id_recv.at[t],
            device_id={"section": right}, device_id_type=MESH,
        )

    def places(t):
        row = idbuf[t].astype(f32)
        i = lax.broadcasted_iota(jnp.int32, (length, length), 0)
        j = lax.broadcasted_iota(jnp.int32, (length, length), 1)
        across = jnp.broadcast_to(row, (length, length))
        down = jnp.sum(jnp.where(i == j, across, 0.0), axis=1, keepdims=True)
        matched = across == down
        place = jnp.sum(jnp.where(matched & (j < i), 1.0, 0.0), axis=1, keepdims=True)
        chosen = jnp.where(j.astype(f32) == place, 1.0, 0.0).astype(bf)
        made = jnp.dot(chosen, table[...], preferred_element_type=f32)
        turns[:, :HD] = made[:, :HD] + made[:, 2 * HD : 3 * HD]
        turns[:, HD:] = made[:, HD : 2 * HD] + made[:, 3 * HD :]
        limits = jnp.where(matched & (j <= i), 0.0, -1e30)
        for r0, r1, k0, k1 in blocks[0] + blocks[1]:
            bias[r0:r1, :] = limits[r0:r1, k0:k1]

    def weigh(t, start, stop):
        rows = slice(start, stop)
        x = xbuf[t, rows, :].astype(f32)
        normed[rows, :] = (x * gain[...].astype(f32)).astype(bf)
        mean = jnp.sum(x * x, axis=1, keepdims=True) * (1.0 / width)
        s = jnp.broadcast_to(lax.rsqrt(mean + 1e-05), (stop - start, HD))
        scale[rows, :] = s
        c, d = turns[rows, :HD] * s, turns[rows, HD:] * s
        cosk[rows, :] = c
        sink[rows, :] = d
        cosq[rows, :] = c * FOLD
        sinq[rows, :] = d * FOLD

    def keep(j, start, stop):
        rows = slice(start, stop)

        def turn(x, cosine, sine):
            return (x * cosine[rows, :] + pltpu.roll(x, HD // 2, 1) * sine[rows, :]).astype(bf)

        for c in range(4):
            made = jnp.dot(
                normed[rows, :], wqkv[j, :, c * 2 * HD : (c + 1) * 2 * HD], preferred_element_type=f32
            )
            a, b = made[:, :HD], made[:, HD:]
            if c < 2:
                at = slice(c * HD, (c + 1) * HD)
                qs[j, 0, rows, at] = turn(a, cosq, sinq)
                qs[j, 1, rows, at] = turn(b, cosq, sinq)
            elif c == 2:
                kd[j, 0, rows, :HD] = turn(a, cosk, sink)
                kd[j, 1, rows, HD:] = turn(b, cosk, sink)
            else:
                vd[j, 0, rows, :HD] = (a * scale[rows, :]).astype(bf)
                vd[j, 1, rows, HD:] = (b * scale[rows, :]).astype(bf)

    def score(j, over):
        made = []
        for r0, r1, k0, k1 in over:
            count = r1 - r0
            q = qs[j, :, r0:r1, :].reshape(2 * count, 2 * HD)
            keys = kd[j, :, k0:k1, :].reshape(2 * HD, 2 * HD)
            scores = lax.dot_general(q, keys, (((1,), (1,)), ((), ())), preferred_element_type=f32)
            limit = bias[r0:r1, :]
            limit = jnp.concatenate([limit, limit], axis=0)
            parts = []
            for h in range(2):
                expo = jnp.exp2(scores[:, h * HD : (h + 1) * HD] + limit)
                parts.append((expo * pl.reciprocal(jnp.sum(expo, axis=1, keepdims=True))).astype(bf))
            made.append(jnp.concatenate(parts, axis=1))
        return made

    def mix(j, over, made):
        for (r0, r1, k0, k1), shares in zip(over, made):
            count = r1 - r0
            values = vd[j, :, k0:k1, :].reshape(2 * HD, 2 * HD)
            got = jnp.dot(shares, values, preferred_element_type=f32).astype(bf)
            for g in range(2):
                for h in range(2):
                    at = (4 * j + 2 * g + h) * HD
                    mixed[r0:r1, at : at + HD] = got[h * count : (h + 1) * count, g * HD : (g + 1) * HD]

    def spread(j, start, stop):
        rows, at = slice(start, stop), slice(j * 4 * HD, (j + 1) * 4 * HD)
        for p in range(PIECES):
            cols = slice(p * piece, (p + 1) * piece)
            made = jnp.dot(mixed[rows, at], wout[at, cols], preferred_element_type=f32)
            if j == 0:
                oacc[rows, cols] = made
            else:
                oacc[rows, cols] += made

    def finish(t, start, stop, first):
        rows = slice(start, stop)
        for p in range(PIECES):
            cols = slice(p * piece, (p + 1) * piece)
            update = jnp.dot(mixed[rows, first:], wout[first:, cols], preferred_element_type=f32)
            if first:
                update += oacc[rows, cols]
            ybuf[t, rows, cols] = (xbuf[t, rows, cols].astype(f32) + update).astype(bf)

    def arrive(j):
        for copy in pair_copies(j):
            copy.wait()

    both = blocks[0] + blocks[1]
    places(0)
    weigh(0, 0, length)
    arrive(0)
    issue(2)
    keep(0, 0, length)
    arrive(1)
    pl.semaphore_wait(barrier, 1)
    id_copy(0).start()
    issue(3)
    out_copy(0).start()
    out_copy(1).start()
    out_copy(2).start()
    out_copy(3).start()
    keep(1, 0, length)
    low0 = score(0, blocks[0])
    arrive(2)
    keep(2, 0, length)
    low1 = score(1, blocks[0])
    mix(0, blocks[0], low0)
    high0 = score(0, blocks[1])
    arrive(3)
    keep(3, 0, length)
    low2 = score(2, blocks[0])
    mix(1, blocks[0], low1)
    high1 = score(1, blocks[1])
    low3 = score(3, blocks[0])
    mix(2, blocks[0], low2)
    mix(3, blocks[0], low3)
    out_copy(0).wait()
    out_copy(1).wait()
    out_copy(2).wait()
    out_copy(3).wait()
    finish(0, *halves[0], 0)
    half_copy(0, 0).start()
    mix(0, blocks[1], high0)
    mix(1, blocks[1], high1)
    high2 = score(2, blocks[1])
    high3 = score(3, blocks[1])
    mix(2, blocks[1], high2)
    mix(3, blocks[1], high3)
    finish(0, *halves[1], 0)
    half_copy(0, 1).start()

    def later(t, carry):
        id_copy(t - 1).wait_recv()

        @pl.when(t < TICKS - 1)
        def _():
            id_copy(t).start()

        places(t)
        for h, (start, stop) in enumerate(halves):
            over = blocks[h]
            half_copy(t - 1, h).wait_recv()
            weigh(t, start, stop)
            keep(0, start, stop)
            keep(1, start, stop)
            made0 = score(0, over)
            keep(2, start, stop)
            mix(0, over, made0)
            made1 = score(1, over)
            keep(3, start, stop)
            mix(1, over, made1)
            made2 = score(2, over)
            spread(0, start, stop)
            mix(2, over, made2)
            made3 = score(3, over)
            spread(1, start, stop)
            spread(2, start, stop)
            mix(3, over, made3)
            finish(t, start, stop, (PAIRS - 1) * 4 * HD)
            pl.when(t < TICKS - 1)(half_copy(t, h).start)
        return carry

    lax.fori_loop(1, TICKS, later, 0)
    out[0] = ybuf[TICKS - 1]
    for t in range(TICKS - 1):
        id_copy(t).wait_send()
        for h in range(2):
            half_copy(t, h).wait_send()


def body(micro, segment, gain, w_query, w_key, w_value, w_out):
    _, length, width = micro.shape
    table = jnp.asarray(rope_table(length))
    bf, f32 = jnp.bfloat16, jnp.float32
    any_space = pl.BlockSpec(memory_space=pl.ANY)
    vmem = pl.BlockSpec(memory_space=pltpu.VMEM)
    return pl.pallas_call(
        functools.partial(kernel, length, width),
        out_shape=jax.ShapeDtypeStruct((1, length, width), bf),
        in_specs=[any_space] * 8,
        out_specs=vmem,
        scratch_shapes=[
            pltpu.VMEM((TICKS, length, width), bf),
            pltpu.VMEM((TICKS, length, width), bf),
            pltpu.VMEM((TICKS, 1, length), jnp.int32),
            pltpu.VMEM((1, width), bf),
            pltpu.VMEM(table.shape, bf),
            pltpu.VMEM((PAIRS, width, 8 * HD), bf),
            pltpu.VMEM((PAIRS * 4 * HD, width), bf),
            pltpu.VMEM((length, width), bf),
            pltpu.VMEM((length, width), f32),
            pltpu.VMEM((PAIRS, 2, length, 2 * HD), bf),
            pltpu.VMEM((PAIRS, 2, length, 2 * HD), bf),
            pltpu.VMEM((PAIRS, 2, length, 2 * HD), bf),
            pltpu.VMEM((length, PAIRS * 4 * HD), bf),
            pltpu.VMEM((length, 2 * HD), f32),
            pltpu.VMEM((length, HD), f32),
            pltpu.VMEM((length, HD), f32),
            pltpu.VMEM((length, HD), f32),
            pltpu.VMEM((length, HD), f32),
            pltpu.VMEM((length, HD), f32),
            pltpu.VMEM((length, HD), f32),
            pltpu.SemaphoreType.DMA((PAIRS, 3)),
            pltpu.SemaphoreType.DMA((PIECES,)),
            pltpu.SemaphoreType.DMA((4,)),
            pltpu.SemaphoreType.DMA((TICKS - 1, 2)),
            pltpu.SemaphoreType.DMA((TICKS - 1, 2)),
            pltpu.SemaphoreType.DMA((TICKS - 1,)),
            pltpu.SemaphoreType.DMA((TICKS - 1,)),
        ],
        compiler_params=pltpu.CompilerParams(
            collective_id=0, has_side_effects=True, vmem_limit_bytes=44 * 1024 * 1024
        ),
    )(*[pltpu.with_memory_space_constraint(a, pltpu.HBM) for a in (micro, segment, gain, table, w_query, w_key, w_value, w_out)])


def solution(mesh):
    in_specs = (
        P(("groups", "section"), None, None),
        P(("groups", "section"), None),
        P("section", None),
        P("section", None, None),
        P("section", None, None),
        P("section", None, None),
        P("section", None, None),
    )
    out_specs = P(("groups", "section"), None, None)
    return jax.shard_map(body, mesh=mesh, in_specs=in_specs, out_specs=out_specs, check_vma=False)
```
